256 devices in a mesh: row: 32 (over z, x_lo, core), col: 8 (over y, x_hi).
Axes of the slice: x: 4 (x_hi: 2, x_lo: 2; x = x_hi * 2 + x_lo), y: 4, z: 8, core: 2. Of those that a mesh axis runs over, the one named last changes fastest.
Arguments:
- features: bfloat16 [32768, 440], P(('row', 'col')), may hold values from -1 to 1
- coeffs: bfloat16 [32768, 144], P(('row', 'col')), may hold values from -0.125 to 0.125
- targets: float32 [32768, 144], P(('row', 'col')), may hold values from -6 to 6
Outputs:
- residual: float32 [32768, 144], P(('row', 'col'))
The draws below stay inside these ranges and needn't reach their ends.
All inputs are finite; a program needn't handle non-finite values.
Results may differ from the reference program's by a relative error of at most 0.0012.
Values may be sent and summed in bfloat16 or wider, within the bound.
A program may use at most 64 MiB of HBM per device.

```python
import math
import jax
import jax.numpy as jnp
from jax import lax

FEAT = 440
OUTS = 144
FRAMES = 32768


def draw_features(key, part):
    clusters = math.gcd(32, FRAMES)
    members = FRAMES // clusters
    streams = jax.random.split(jax.random.fold_in(key, 7301), 7)
    centre_basis = jax.random.normal(streams[0], (8, FEAT), jnp.float32) / math.sqrt(FEAT)
    local_basis = jax.random.normal(streams[1], (clusters, 16, FEAT), jnp.float32) / math.sqrt(FEAT)
    centre_coords = jax.random.normal(streams[2], (clusters, 8), jnp.float32) * 0.9
    spread = jnp.exp(jax.random.uniform(streams[3], (clusters, 1, 1), jnp.float32, math.log(0.04), math.log(0.3)))
    latent = jax.random.normal(streams[4], (clusters, members, 16), jnp.float32) * spread
    noise = jax.random.normal(streams[5], (clusters, members, FEAT), jnp.float32) * 0.01
    centres = jnp.dot(centre_coords, centre_basis)
    local = jnp.einsum('cmk,ckf->cmf', latent, local_basis)
    frames = (centres[:, None, :] + local + noise).reshape(FRAMES, FEAT)
    order = jax.random.permutation(streams[6], FRAMES)
    frames = frames[order]
    return jnp.clip(frames, -1.0, 1.0).astype(jnp.bfloat16)


def level_of(own_key, extent, pieces, least, high):
    level = 1.0
    for axis_at, shards_of in pieces:
        draws = jax.random.uniform(jax.random.fold_in(jax.random.fold_in(own_key, 6), axis_at), (shards_of,), jnp.float32, least / len(pieces), high / len(pieces))
        level = level * jnp.repeat(jnp.exp(draws), extent[axis_at] // shards_of).reshape((-1,) + (1,) * (len(extent) - 1 - axis_at))
    return level


def normal_values(own_key, extent, width, most, shards=(), held_as=jnp.bfloat16):
    result = jax.random.normal(own_key, extent, jnp.float32) * width
    if len(shards) > 0:
        result = level_of(own_key, extent, shards, -0.22, 0.18) * result
    return jnp.clip(result, min=-most, max=most).astype(held_as)


def setup_inputs(seed: int = 0) -> dict:
    key_list = jax.random.split(jax.random.key(seed), 4)
    return {
        "features": draw_features(jax.random.fold_in(key_list[3], 71), 0),
        "coeffs": normal_values(key_list[1], (FRAMES, OUTS), (FRAMES // 16) ** -0.5, 0.125, ((0, 256),)),
        "targets": normal_values(key_list[2], (FRAMES, OUTS), 1.0, 6.0, ((0, 256),), jnp.float32),
    }


def reference(features, coeffs, targets):
    whole = features.astype(jnp.float32)
    sq = lax.optimization_barrier(jnp.sum(whole * whole, axis=1))
    weights = coeffs.astype(jnp.float32)
    blocks = FRAMES // 1024 if FRAMES % 1024 == 0 else 1
    size = FRAMES // blocks

    def one_block(index):
        start = (index * size).astype(jnp.int32)
        query = lax.dynamic_slice_in_dim(whole, start, size, 0)
        query_sq = lax.dynamic_slice_in_dim(sq, start, size, 0)
        inner = jnp.dot(query, whole.T, precision=lax.Precision.HIGHEST)
        dist = jnp.sqrt(jnp.maximum(query_sq[:, None] + sq[None, :] - 2.0 * inner, 0.0))
        kernel = jnp.exp(-dist).astype(jnp.bfloat16).astype(jnp.float32)
        return jnp.dot(kernel, weights, precision=lax.Precision.HIGHEST)
    parts = lax.map(one_block, jnp.arange(blocks, dtype=jnp.int32))
    return parts.reshape(FRAMES, OUTS) - targets
```

```python
import functools

import jax
import jax.numpy as jnp
from jax import lax
from jax.experimental import pallas as pl
from jax.experimental.pallas import tpu as pltpu
from jax.sharding import PartitionSpec as P

MESH = pl.DeviceIdType.MESH
NX, NY, NZ = 4, 4, 8
FEAT, OUTS, OWN = 440, 144, 128
PAD = 512
WIRE = 448
HEAD = 64
PIECES = 5
LOG2E = 1.4426950408889634


def contract(a, b):
    return lax.dot_general(a, b, (((1,), (0,)), ((), ())), preferred_element_type=jnp.float32)


def laplacian(squared):
    squared = jnp.maximum(squared, 1e-30)
    return jnp.exp2((squared * -LOG2E) * lax.rsqrt(squared)).astype(jnp.bfloat16)


def kernel(
    feat_hbm, coef_hbm, out_ref,
    feat, coef, cols, weights, rows, gram, sent, inbox, own_sum,
    load_sem, z_send, z_recv, chip_send, chip_recv, p_send, q_send, relay_send, row_recv, out_send, out_recv,
):
    row, col = lax.axis_index("row"), lax.axis_index("col")
    z, core = row // 4, row % 2
    x, y = (col % 2) * 2 + (row // 2) % 2, col // 2
    flip = 1 - core

    def device(x, y, z, core):
        return (z * 4 + (x % 2) * 2 + core, y * 2 + x // 2)

    def plane(a, b):
        return device((x + flip * a + core * b) % NX, (y + core * a + flip * b) % NY, z, core)

    def line(step):
        return device(x, y, (z + step + NZ) % NZ, core)

    sibling = device(x, y, z, flip)

    barrier = pltpu.get_barrier_semaphore()
    near = [line(1), line(-1), sibling, plane(1, 0), plane(3, 0), plane(2, 0), plane(0, 1), plane(0, 3)]
    for peer in near:
        pl.semaphore_signal(barrier, inc=1, device_id=peer, device_id_type=MESH)

    load_feat = pltpu.make_async_copy(feat_hbm, feat, load_sem.at[0])
    load_coef = pltpu.make_async_copy(coef_hbm, coef, load_sem.at[1])
    load_feat.start()
    load_coef.start()

    @pl.loop(1, 16)
    def _(slot):
        rows[slot, WIRE:PAD, :] = jnp.zeros((PAD - WIRE, OWN), jnp.bfloat16)

    load_feat.wait()
    load_coef.wait()

    low = feat[:, 0:384].astype(jnp.float32)
    high = feat[:, 384:FEAT].astype(jnp.float32)
    square = jnp.sum(low * low, axis=1, keepdims=True) + jnp.sum(high * high, axis=1, keepdims=True)
    first = square.astype(jnp.bfloat16).astype(jnp.float32)
    second = (square - first).astype(jnp.bfloat16).astype(jnp.float32)
    third = square - first - second
    lane = lax.broadcasted_iota(jnp.int32, (OWN, 128), 1)
    high = jnp.concatenate([high, jnp.zeros((OWN, 128 - high.shape[1]), jnp.float32)], axis=1)
    coef_low = coef[:, 0:128].astype(jnp.float32)
    coef_high = jnp.concatenate([coef[:, 128:OUTS].astype(jnp.float32), jnp.zeros((OWN, 256 - OUTS), jnp.float32)], axis=1)
    pieces = jnp.where(lane % 3 == 2, first, jnp.where(lane % 3 == 0, second, third))
    ones = jnp.ones((OWN, 128), jnp.float32)
    nothing = jnp.zeros((OWN, 128), jnp.float32)
    column_tail = jnp.where(lane < 56, high * -2.0, jnp.where(lane < 59, pieces, jnp.where(lane < 62, ones, nothing)))
    column_tail = jnp.where(lane < 64, column_tail, pltpu.roll(coef_low, 64, 1))
    row_tail = jnp.where(lane < 56, high, jnp.where(lane < 59, ones, jnp.where(lane < 62, pieces, nothing)))
    cols[0, :, 0:384] = (low * -2.0).astype(jnp.bfloat16)
    cols[0, :, 384:PAD] = column_tail.astype(jnp.bfloat16)
    for t in range(3):
        rows[0, t * 128 : (t + 1) * 128, :] = jnp.transpose(low[:, t * 128 : (t + 1) * 128]).astype(jnp.bfloat16)
    rows[0, 384:PAD, :] = jnp.transpose(row_tail).astype(jnp.bfloat16)
    weights[0, 0:128, :] = jnp.transpose(coef_low).astype(jnp.bfloat16)
    weights[0, 128:OUTS, :] = jnp.transpose(coef_high)[0 : OUTS - 128].astype(jnp.bfloat16)

    pl.semaphore_wait(barrier, len(near))

    started = []

    def send(src, dst, send_sem, recv_sem, peer):
        copy = pltpu.make_async_remote_copy(
            src_ref=src, dst_ref=dst, send_sem=send_sem, recv_sem=recv_sem, device_id=peer, device_id_type=MESH
        )
        copy.start()
        started.append(copy)

    def arrived(dst, recv_sem):
        pltpu.make_async_remote_copy(
            src_ref=dst, dst_ref=dst, send_sem=load_sem.at[0], recv_sem=recv_sem, device_id=sibling, device_id_type=MESH
        ).wait_recv()

    def part(slot, piece):
        if piece < 4:
            return cols.at[slot, pl.ds(32 * piece, 32), :]
        return weights.at[slot, pl.ds(HEAD, OUTS - HEAD), :]

    def z_hop(step, piece, up):
        src = (8 - step + 1) % 8 if up else step - 1
        dst = 8 - step if up else step
        send(
            part(2 * src, piece), part(2 * dst, piece),
            z_send.at[int(up), step - 1, piece], z_recv.at[dst, piece], line(1 if up else -1),
        )

    def z_arrived(dz, piece):
        arrived(part(2 * dz, piece), z_recv.at[dz, piece])

    def to_sibling(dz):
        send(cols.at[2 * dz], cols.at[2 * dz + 1], chip_send.at[dz, 0], chip_recv.at[dz, 0], sibling)
        send(part(2 * dz, 4), part(2 * dz + 1, 4), chip_send.at[dz, 1], chip_recv.at[dz, 1], sibling)

    def from_sibling(dz):
        arrived(cols.at[2 * dz + 1], chip_recv.at[dz, 0])
        arrived(part(2 * dz + 1, 4), chip_recv.at[dz, 1])

    def row_block(a, b):
        return rows.at[4 * b + a, pl.ds(0, WIRE), :]

    def send_row(a, b, to_a, to_b, send_sem):
        there = ((a - to_a) % 4, (b - to_b) % 4)
        send(row_block(a, b), row_block(*there), send_sem, row_recv.at[4 * there[1] + there[0]], plane(to_a, to_b))

    def row_arrived(a, b):
        arrived(row_block(a, b), row_recv.at[4 * b + a])

    def across(a):
        send_row(a, 0, 0, 1, q_send.at[0, a])
        send_row(a, 0, 0, 3, q_send.at[1, a])

    def relay(a):
        if a < 2:
            row_arrived(a, 3)
            send_row(a, 3, 0, 1, relay_send.at[a])
        else:
            row_arrived(a, 1)
            send_row(a, 1, 0, 3, relay_send.at[a])

    def head_rows(slot):
        tail = jnp.transpose(cols[slot, :, 384:PAD].astype(jnp.float32))
        weights[slot, 0:HEAD, :] = tail[HEAD:128].astype(jnp.bfloat16)

    for piece in range(PIECES):
        for up in (True, False):
            z_hop(1, piece, up)
        if piece == 0:
            for a in (1, 3):
                send_row(0, 0, a, 0, p_send.at[a])
            across(0)
            send_row(0, 0, 2, 0, p_send.at[2])
    to_sibling(0)

    def z_round(step, pieces):
        for piece in pieces:
            for up in (True, False):
                z_arrived(8 - step if up else step, piece)
                if step < 3 or (step == 3 and (piece < 2) == up):
                    z_hop(step + 1, piece, up)

    z_round(1, (0, 1, 2))
    for a in (1, 3):
        row_arrived(a, 0)
        across(a)
    relay(0)
    z_round(1, (3, 4))
    to_sibling(1)
    to_sibling(7)
    row_arrived(2, 0)
    across(2)
    z_round(2, (0, 1))
    relay(1)
    relay(3)
    z_round(2, (2, 3, 4))
    to_sibling(2)
    to_sibling(6)
    relay(2)
    from_sibling(0)
    for dz in (1, 7):
        from_sibling(dz)
        head_rows(2 * dz)
        head_rows(2 * dz + 1)
    head_rows(1)
    z_round(3, range(5))
    to_sibling(3)
    to_sibling(5)
    for dz in (2, 6):
        from_sibling(dz)
        head_rows(2 * dz)
        head_rows(2 * dz + 1)
    for piece in range(5):
        z_arrived(4, piece)
    to_sibling(4)
    for dz in (3, 5, 4):
        head_rows(2 * dz)
        from_sibling(dz)
        head_rows(2 * dz + 1)
    for a, b in ((0, 1), (1, 1), (3, 3), (2, 3), (0, 2), (1, 2), (2, 2), (3, 2)):
        row_arrived(a, b)

    all_weights = jnp.concatenate([weights[slot] for slot in range(16)], axis=1)

    def out_copy(a, b):
        slot = 4 * b + a
        return pltpu.make_async_remote_copy(
            src_ref=sent.at[slot], dst_ref=inbox.at[slot], send_sem=out_send.at[slot], recv_sem=out_recv.at[slot],
            device_id=plane(a, b), device_id_type=MESH,
        )

    @pl.loop(0, 4)
    def _(b):
        group = jnp.concatenate([rows[4 * b + a] for a in range(4)], axis=1)
        for slot in range(0, 16, 2):
            block = cols[slot : slot + 2].reshape(2 * OWN, PAD)
            gram[slot * OWN : (slot + 2) * OWN, :] = laplacian(contract(block, group))
        total = contract(all_weights, gram[...])

        @pl.when(b == 0)
        def _():
            own_sum[...] = total[:, 0:OWN]

        for a in range(4):
            sent[4 * b + a] = total[:, a * OWN : (a + 1) * OWN].astype(jnp.bfloat16)
        for a in range(4):
            if a == 0:
                @pl.when(b > 0)
                def _():
                    out_copy(0, b).start()
            else:
                out_copy(a, b).start()

    total = own_sum[...]
    for slot in range(1, 16):
        arrived(inbox.at[slot], out_recv.at[slot])
        total = total + inbox[slot].astype(jnp.float32)
    out_ref[:, 0:128] = jnp.transpose(total[0:128])
    rest = jnp.concatenate([total[128:OUTS], jnp.zeros((256 - OUTS, OWN), jnp.float32)], axis=0)
    out_ref[:, 128:OUTS] = jnp.transpose(rest)[:, 0 : OUTS - 128]

    for copy in started:
        copy.wait_send()
    for slot in range(1, 16):
        out_copy(slot % 4, slot // 4).wait_send()


def per_device(features, coeffs, targets):
    dma = pltpu.SemaphoreType.DMA
    predicted = pl.pallas_call(
        kernel,
        out_shape=jax.ShapeDtypeStruct((OWN, OUTS), jnp.float32),
        in_specs=[pl.BlockSpec(memory_space=pl.ANY)] * 2,
        out_specs=pl.BlockSpec(memory_space=pltpu.VMEM),
        scratch_shapes=[
            pltpu.VMEM((OWN, FEAT), jnp.bfloat16),
            pltpu.VMEM((OWN, OUTS), jnp.bfloat16),
            pltpu.VMEM((16, OWN, PAD), jnp.bfloat16),
            pltpu.VMEM((16, OUTS, OWN), jnp.bfloat16),
            pltpu.VMEM((16, PAD, OWN), jnp.bfloat16),
            pltpu.VMEM((16 * OWN, 4 * OWN), jnp.bfloat16),
            pltpu.VMEM((16, OUTS, OWN), jnp.bfloat16),
            pltpu.VMEM((16, OUTS, OWN), jnp.bfloat16),
            pltpu.VMEM((OUTS, OWN), jnp.float32),
            dma((2,)),
            dma((2, 4, PIECES)), dma((8, PIECES)),
            dma((8, 2)), dma((8, 2)),
            dma((4,)), dma((2, 4)), dma((4,)), dma((16,)),
            dma((16,)), dma((16,)),
        ],
        compiler_params=pltpu.CompilerParams(collective_id=0, has_side_effects=True, vmem_limit_bytes=48 << 20),
        name="ridge",
    )(features, coeffs)
    return predicted - targets


def solution(mesh):
    spec = P(("row", "col"), None)
    return jax.shard_map(per_device, mesh=mesh, in_specs=(spec, spec, spec), out_specs=spec, check_vma=False)
```

```python
import functools

import jax
import jax.numpy as jnp
from jax import lax
from jax.experimental import pallas as pl
from jax.experimental.pallas import tpu as pltpu
from jax.sharding import PartitionSpec as P

MESH = pl.DeviceIdType.MESH
NX, NY, NZ = 4, 4, 8
FEAT, OUTS, OWN = 440, 144, 128
PAD = 512
WIRE = 448
HEAD = 64
PIECES = 5
LOG2E = 1.4426950408889634


def contract(a, b):
    return lax.dot_general(a, b, (((1,), (0,)), ((), ())), preferred_element_type=jnp.float32)


def laplacian(squared):
    squared = jnp.maximum(squared, 1e-30)
    return jnp.exp2((squared * -LOG2E) * lax.rsqrt(squared)).astype(jnp.bfloat16)


def kernel(
    feat_hbm, coef_hbm, out_ref,
    feat, coef, cols, weights, rows, gram, sums, sent, inbox, own_sum,
    load_sem, z_send, z_recv, chip_send, chip_recv, p_send, q_send, relay_send, row_recv, out_send, out_recv,
):
    row, col = lax.axis_index("row"), lax.axis_index("col")
    z, core = row // 4, row % 2
    x, y = (col % 2) * 2 + (row // 2) % 2, col // 2
    flip = 1 - core

    def device(x, y, z, core):
        return (z * 4 + (x % 2) * 2 + core, y * 2 + x // 2)

    def plane(a, b):
        return device((x + flip * a + core * b) % NX, (y + core * a + flip * b) % NY, z, core)

    def line(step):
        return device(x, y, (z + step + NZ) % NZ, core)

    sibling = device(x, y, z, flip)

    barrier = pltpu.get_barrier_semaphore()
    near = [line(1), line(-1), sibling, plane(1, 0), plane(3, 0), plane(2, 0), plane(0, 1), plane(0, 3)]
    for peer in near:
        pl.semaphore_signal(barrier, inc=1, device_id=peer, device_id_type=MESH)

    load_feat = pltpu.make_async_copy(feat_hbm, feat, load_sem.at[0])
    load_coef = pltpu.make_async_copy(coef_hbm, coef, load_sem.at[1])
    load_feat.start()
    load_coef.start()

    @pl.loop(1, 16)
    def _(slot):
        rows[slot, WIRE:PAD, :] = jnp.zeros((PAD - WIRE, OWN), jnp.bfloat16)

    load_feat.wait()
    load_coef.wait()

    values = feat[...].astype(jnp.float32)
    head = coef[0:HEAD, :].astype(jnp.float32)
    square = jnp.sum(values * values, axis=0, keepdims=True)
    first = square.astype(jnp.bfloat16).astype(jnp.float32)
    second = (square - first).astype(jnp.bfloat16).astype(jnp.float32)
    third = square - first - second
    at = lax.broadcasted_iota(jnp.int32, (8, OWN), 0)
    pieces = jnp.where(at % 3 == 0, first, jnp.where(at % 3 == 1, second, third))
    column_extra = jnp.where(at < 3, pieces, jnp.where(at < 6, 1.0, 0.0))
    row_extra = jnp.where(at < 3, 1.0, jnp.where(at < 6, pieces, 0.0))
    by_rows = jnp.concatenate([values, row_extra, jnp.zeros_like(head)], axis=0)
    rows[0] = by_rows.astype(jnp.bfloat16)
    by_columns = jnp.concatenate([values * -2.0, column_extra, head], axis=0)
    for t in range(4):
        cols[0, :, t * 128 : (t + 1) * 128] = jnp.transpose(by_columns[t * 128 : (t + 1) * 128]).astype(jnp.bfloat16)
    weights[0] = coef[...]

    pl.semaphore_wait(barrier, len(near))

    started = []

    def send(src, dst, send_sem, recv_sem, peer):
        copy = pltpu.make_async_remote_copy(
            src_ref=src, dst_ref=dst, send_sem=send_sem, recv_sem=recv_sem, device_id=peer, device_id_type=MESH
        )
        copy.start()
        started.append(copy)

    def arrived(dst, recv_sem):
        pltpu.make_async_remote_copy(
            src_ref=dst, dst_ref=dst, send_sem=load_sem.at[0], recv_sem=recv_sem, device_id=sibling, device_id_type=MESH
        ).wait_recv()

    def part(slot, piece):
        if piece < 4:
            return cols.at[slot, pl.ds(32 * piece, 32), :]
        return weights.at[slot, pl.ds(HEAD, OUTS - HEAD), :]

    def z_hop(step, piece, up):
        src = (8 - step + 1) % 8 if up else step - 1
        dst = 8 - step if up else step
        send(
            part(2 * src, piece), part(2 * dst, piece),
            z_send.at[int(up), step - 1, piece], z_recv.at[dst, piece], line(1 if up else -1),
        )

    def z_arrived(dz, piece):
        arrived(part(2 * dz, piece), z_recv.at[dz, piece])

    def to_sibling(dz):
        send(cols.at[2 * dz], cols.at[2 * dz + 1], chip_send.at[dz, 0], chip_recv.at[dz, 0], sibling)
        send(part(2 * dz, 4), part(2 * dz + 1, 4), chip_send.at[dz, 1], chip_recv.at[dz, 1], sibling)

    def from_sibling(dz):
        arrived(cols.at[2 * dz + 1], chip_recv.at[dz, 0])
        arrived(part(2 * dz + 1, 4), chip_recv.at[dz, 1])

    def row_block(a, b):
        return rows.at[4 * b + a, pl.ds(0, WIRE), :]

    def send_row(a, b, to_a, to_b, send_sem):
        there = ((a - to_a) % 4, (b - to_b) % 4)
        send(row_block(a, b), row_block(*there), send_sem, row_recv.at[4 * there[1] + there[0]], plane(to_a, to_b))

    def row_arrived(a, b):
        arrived(row_block(a, b), row_recv.at[4 * b + a])

    def across(a):
        send_row(a, 0, 0, 1, q_send.at[0, a])
        send_row(a, 0, 0, 3, q_send.at[1, a])

    def relay(a):
        if a < 2:
            row_arrived(a, 3)
            send_row(a, 3, 0, 1, relay_send.at[a])
        else:
            row_arrived(a, 1)
            send_row(a, 1, 0, 3, relay_send.at[a])

    def head_rows(slot):
        tail = jnp.transpose(cols[slot, :, 384:PAD].astype(jnp.float32))
        weights[slot, 0:HEAD, :] = tail[HEAD:128].astype(jnp.bfloat16)

    for piece in range(PIECES):
        for up in (True, False):
            z_hop(1, piece, up)
        if piece == 0:
            for a in (1, 3):
                send_row(0, 0, a, 0, p_send.at[a])
            across(0)
            send_row(0, 0, 2, 0, p_send.at[2])
    to_sibling(0)

    def z_round(step, pieces):
        for piece in pieces:
            for up in (True, False):
                z_arrived(8 - step if up else step, piece)
                if step < 3 or (step == 3 and (piece < 2) == up):
                    z_hop(step + 1, piece, up)

    z_round(1, (0, 1, 2))
    for a in (1, 3):
        row_arrived(a, 0)
        across(a)
    relay(0)
    z_round(1, (3, 4))
    to_sibling(1)
    to_sibling(7)
    row_arrived(2, 0)
    across(2)
    z_round(2, (0, 1))
    relay(1)
    relay(3)
    z_round(2, (2, 3, 4))
    to_sibling(2)
    to_sibling(6)
    relay(2)
    from_sibling(0)
    for dz in (1, 7):
        from_sibling(dz)
        head_rows(2 * dz)
        head_rows(2 * dz + 1)
    head_rows(1)
    z_round(3, range(5))
    to_sibling(3)
    to_sibling(5)
    for dz in (2, 6):
        from_sibling(dz)
        head_rows(2 * dz)
        head_rows(2 * dz + 1)

    def against(b, distances):
        group = jnp.concatenate([rows[4 * b + a] for a in range(4)], axis=1)
        for at, dz in enumerate(distances):
            block = cols[2 * dz : 2 * dz + 2].reshape(2 * OWN, PAD)
            gram[2 * at * OWN : 2 * (at + 1) * OWN, :] = laplacian(contract(block, group))
        factors = jnp.concatenate([weights[2 * dz + half] for dz in distances for half in range(2)], axis=1)
        return contract(factors, gram[0 : 2 * len(distances) * OWN, :])

    near_columns, far_columns = (0, 1, 7, 2, 6), (3, 5, 4)
    for a, b in ((0, 1), (1, 1)):
        row_arrived(a, b)

    @pl.loop(0, 2)
    def _(b):
        sums[b] = against(b, near_columns)

    for piece in (0, 2, 1, 3, 4):
        z_arrived(4, piece)
    to_sibling(4)
    for a, b in ((3, 3), (2, 3), (0, 2), (1, 2), (2, 2), (3, 2)):
        row_arrived(a, b)

    @pl.loop(2, 4)
    def _(b):
        sums[b] = against(b, near_columns)

    for dz in (3, 5, 4):
        head_rows(2 * dz)
        from_sibling(dz)
        head_rows(2 * dz + 1)

    def out_copy(a, b):
        slot = 4 * b + a
        return pltpu.make_async_remote_copy(
            src_ref=sent.at[slot], dst_ref=inbox.at[slot], send_sem=out_send.at[slot], recv_sem=out_recv.at[slot],
            device_id=plane(a, b), device_id_type=MESH,
        )

    @pl.loop(0, 4)
    def _(b):
        total = sums[b] + against(b, far_columns)

        @pl.when(b == 0)
        def _():
            own_sum[...] = total[:, 0:OWN]

        for a in range(4):
            sent[4 * b + a] = total[:, a * OWN : (a + 1) * OWN].astype(jnp.bfloat16)
        for a in range(4):
            if a == 0:
                @pl.when(b > 0)
                def _():
                    out_copy(0, b).start()
            else:
                out_copy(a, b).start()

    total = own_sum[...]
    for slot in range(1, 16):
        arrived(inbox.at[slot], out_recv.at[slot])
        total = total + inbox[slot].astype(jnp.float32)
    out_ref[...] = total

    for copy in started:
        copy.wait_send()
    for slot in range(1, 16):
        out_copy(slot % 4, slot // 4).wait_send()


def per_device(features, coeffs, targets):
    dma = pltpu.SemaphoreType.DMA
    predicted = pl.pallas_call(
        kernel,
        out_shape=jax.ShapeDtypeStruct((OUTS, OWN), jnp.float32),
        in_specs=[pl.BlockSpec(memory_space=pl.ANY)] * 2,
        out_specs=pl.BlockSpec(memory_space=pltpu.VMEM),
        scratch_shapes=[
            pltpu.VMEM((FEAT, OWN), jnp.bfloat16),
            pltpu.VMEM((OUTS, OWN), jnp.bfloat16),
            pltpu.VMEM((16, OWN, PAD), jnp.bfloat16),
            pltpu.VMEM((16, OUTS, OWN), jnp.bfloat16),
            pltpu.VMEM((16, PAD, OWN), jnp.bfloat16),
            pltpu.VMEM((10 * OWN, 4 * OWN), jnp.bfloat16),
            pltpu.VMEM((4, OUTS, 4 * OWN), jnp.float32),
            pltpu.VMEM((16, OUTS, OWN), jnp.bfloat16),
            pltpu.VMEM((16, OUTS, OWN), jnp.bfloat16),
            pltpu.VMEM((OUTS, OWN), jnp.float32),
            dma((2,)),
            dma((2, 4, PIECES)), dma((8, PIECES)),
            dma((8, 2)), dma((8, 2)),
            dma((4,)), dma((2, 4)), dma((4,)), dma((16,)),
            dma((16,)), dma((16,)),
        ],
        compiler_params=pltpu.CompilerParams(collective_id=0, has_side_effects=True, vmem_limit_bytes=60 << 20),
        name="ridge",
    )(features.T, coeffs.T)
    return predicted.T - targets


def solution(mesh):
    spec = P(("row", "col"), None)
    return jax.shard_map(per_device, mesh=mesh, in_specs=(spec, spec, spec), out_specs=spec, check_vma=False)
```

```python
import functools

import jax
import jax.numpy as jnp
from jax import lax
from jax.experimental import pallas as pl
from jax.experimental.pallas import tpu as pltpu
from jax.sharding import PartitionSpec as P

MESH = pl.DeviceIdType.MESH
NX, NY, NZ = 4, 4, 8
FEAT, OUTS, OWN = 440, 144, 128
PAD = 512
WIRE = 448
HEAD = 64
PIECES = 5
LOG2E = 1.4426950408889634


def contract(a, b):
    return lax.dot_general(a, b, (((1,), (0,)), ((), ())), preferred_element_type=jnp.float32)


def laplacian(squared):
    squared = jnp.maximum(squared, 1e-30)
    return jnp.exp2((squared * -LOG2E) * lax.rsqrt(squared)).astype(jnp.bfloat16)


def kernel(
    feat_hbm, coef_hbm, out_ref,
    feat, coef, cols, weights, rows, gram, sums, sent, inbox,
    load_sem, z_send, z_recv, chip_send, chip_recv, p_send, q_send, relay_send, row_recv, out_send, out_recv,
):
    row, col = lax.axis_index("row"), lax.axis_index("col")
    z, core = row // 4, row % 2
    x, y = (col % 2) * 2 + (row // 2) % 2, col // 2
    flip = 1 - core

    def device(x, y, z, core):
        return (z * 4 + (x % 2) * 2 + core, y * 2 + x // 2)

    def plane(a, b):
        return device((x + flip * a + core * b) % NX, (y + core * a + flip * b) % NY, z, core)

    def line(step):
        return device(x, y, (z + step + NZ) % NZ, core)

    sibling = device(x, y, z, flip)

    barrier = pltpu.get_barrier_semaphore()
    near = [line(1), line(-1), sibling, plane(1, 0), plane(3, 0), plane(2, 0), plane(0, 1), plane(0, 3)]
    for peer in near:
        pl.semaphore_signal(barrier, inc=1, device_id=peer, device_id_type=MESH)

    load_feat = pltpu.make_async_copy(feat_hbm, feat, load_sem.at[0])
    load_coef = pltpu.make_async_copy(coef_hbm, coef, load_sem.at[1])
    load_feat.start()
    load_coef.start()

    @pl.loop(1, 16)
    def _(slot):
        rows[slot, WIRE:PAD, :] = jnp.zeros((PAD - WIRE, OWN), jnp.bfloat16)

    load_feat.wait()
    load_coef.wait()

    values = feat[...].astype(jnp.float32)
    head = coef[0:HEAD, :].astype(jnp.float32)
    square = jnp.sum(values * values, axis=0, keepdims=True)
    first = square.astype(jnp.bfloat16).astype(jnp.float32)
    second = (square - first).astype(jnp.bfloat16).astype(jnp.float32)
    third = square - first - second
    at = lax.broadcasted_iota(jnp.int32, (8, OWN), 0)
    pieces = jnp.where(at % 3 == 0, first, jnp.where(at % 3 == 1, second, third))
    column_extra = jnp.where(at < 3, pieces, jnp.where(at < 6, 1.0, 0.0))
    row_extra = jnp.where(at < 3, 1.0, jnp.where(at < 6, pieces, 0.0))
    by_rows = jnp.concatenate([values, row_extra, jnp.zeros_like(head)], axis=0)
    rows[0] = by_rows.astype(jnp.bfloat16)
    by_columns = jnp.concatenate([values * -2.0, column_extra, head], axis=0)
    for t in range(4):
        cols[0, :, t * 128 : (t + 1) * 128] = jnp.transpose(by_columns[t * 128 : (t + 1) * 128]).astype(jnp.bfloat16)
    weights[0] = coef[...]

    pl.semaphore_wait(barrier, len(near))

    started = []

    def send(src, dst, send_sem, recv_sem, peer):
        copy = pltpu.make_async_remote_copy(
            src_ref=src, dst_ref=dst, send_sem=send_sem, recv_sem=recv_sem, device_id=peer, device_id_type=MESH
        )
        copy.start()
        started.append(copy)

    def arrived(dst, recv_sem):
        pltpu.make_async_remote_copy(
            src_ref=dst, dst_ref=dst, send_sem=load_sem.at[0], recv_sem=recv_sem, device_id=sibling, device_id_type=MESH
        ).wait_recv()

    def part(slot, piece):
        if piece < 4:
            return cols.at[slot, pl.ds(32 * piece, 32), :]
        return weights.at[slot, pl.ds(HEAD, OUTS - HEAD), :]

    def z_hop(step, piece, up):
        src = (8 - step + 1) % 8 if up else step - 1
        dst = 8 - step if up else step
        send(
            part(2 * src, piece), part(2 * dst, piece),
            z_send.at[int(up), step - 1, piece], z_recv.at[dst, piece], line(1 if up else -1),
        )

    def z_arrived(dz, piece):
        arrived(part(2 * dz, piece), z_recv.at[dz, piece])

    def to_sibling(dz):
        send(cols.at[2 * dz], cols.at[2 * dz + 1], chip_send.at[dz, 0], chip_recv.at[dz, 0], sibling)
        send(part(2 * dz, 4), part(2 * dz + 1, 4), chip_send.at[dz, 1], chip_recv.at[dz, 1], sibling)

    def from_sibling(dz):
        arrived(cols.at[2 * dz + 1], chip_recv.at[dz, 0])
        arrived(part(2 * dz + 1, 4), chip_recv.at[dz, 1])

    def row_block(a, b):
        return rows.at[4 * b + a, pl.ds(0, WIRE), :]

    def send_row(a, b, to_a, to_b, send_sem):
        there = ((a - to_a) % 4, (b - to_b) % 4)
        send(row_block(a, b), row_block(*there), send_sem, row_recv.at[4 * there[1] + there[0]], plane(to_a, to_b))

    def row_arrived(a, b):
        arrived(row_block(a, b), row_recv.at[4 * b + a])

    def across(a):
        send_row(a, 0, 0, 1, q_send.at[0, a])
        send_row(a, 0, 0, 3, q_send.at[1, a])

    def relay(a):
        if a < 2:
            row_arrived(a, 3)
            send_row(a, 3, 0, 1, relay_send.at[a])
        else:
            row_arrived(a, 1)
            send_row(a, 1, 0, 3, relay_send.at[a])

    def head_rows(slot):
        tail = jnp.transpose(cols[slot, :, 384:PAD].astype(jnp.float32))
        weights[slot, 0:HEAD, :] = tail[HEAD:128].astype(jnp.bfloat16)

    def against(b, distances):
        group = jnp.concatenate([rows[4 * b + a] for a in range(4)], axis=1)
        for at, dz in enumerate(distances):
            block = cols[2 * dz : 2 * dz + 2].reshape(2 * OWN, PAD)
            gram[2 * at * OWN : 2 * (at + 1) * OWN, :] = laplacian(contract(block, group))
        factors = jnp.concatenate([weights[2 * dz + half] for dz in distances for half in range(2)], axis=1)
        return contract(factors, gram[0 : 2 * len(distances) * OWN, :])

    for piece in range(PIECES):
        for up in (True, False):
            z_hop(1, piece, up)
    for a in (1, 3):
        send_row(0, 0, a, 0, p_send.at[a])
    send_row(0, 0, 2, 0, p_send.at[2])
    across(0)
    to_sibling(0)

    def z_round(step, pieces):
        for piece in pieces:
            for up in (True, False):
                z_arrived(8 - step if up else step, piece)
                if step < 3 or (step == 3 and (piece < 2) == up):
                    z_hop(step + 1, piece, up)

    z_round(1, range(5))
    to_sibling(1)
    to_sibling(7)
    for a in (1, 3):
        row_arrived(a, 0)
        across(a)
    relay(0)
    z_round(2, (0, 1))
    row_arrived(2, 0)
    across(2)
    z_round(2, (2,))
    from_sibling(0)
    head_rows(1)
    sums[0] = against(0, (0,))
    z_round(2, (3, 4))
    to_sibling(2)
    to_sibling(6)
    for dz in (1, 7):
        from_sibling(dz)
        head_rows(2 * dz)
        head_rows(2 * dz + 1)
    z_round(3, (0,))
    sums[0] += against(0, (1,))
    z_round(3, (1,))
    sums[0] += against(0, (7,))
    z_round(3, (2,3, 4))
    relay(1)
    relay(3)
    relay(2)
    to_sibling(3)
    to_sibling(5)
    for dz in (2, 6):
        from_sibling(dz)
        head_rows(2 * dz)
        head_rows(2 * dz + 1)

    near_columns, far_columns = (0, 1, 7, 2, 6), (3, 5, 4)
    for a, b in ((0, 1), (1, 1)):
        row_arrived(a, b)

    sums[0] += against(0, (2, 6))
    sums[1] = against(1, near_columns)

    for piece in (0, 2, 1, 3, 4):
        z_arrived(4, piece)
    to_sibling(4)
    for a, b in ((3, 3), (2, 3)):
        row_arrived(a, b)
    sums[3] = against(3, near_columns)

    for dz in (3, 5, 4):
        head_rows(2 * dz)
        from_sibling(dz)
        head_rows(2 * dz + 1)

    def out_copy(a, b):
        slot = 4 * b + a
        return pltpu.make_async_remote_copy(
            src_ref=sent.at[slot], dst_ref=inbox.at[slot], send_sem=out_send.at[slot], recv_sem=out_recv.at[slot],
            device_id=plane(a, b), device_id_type=MESH,
        )

    def hand_out(b, total, first):
        for a in range(first, 4):
            sent[4 * b + a] = total[:, a * OWN : (a + 1) * OWN].astype(jnp.bfloat16)
        for a in range(first, 4):
            out_copy(a, b).start()

    @pl.loop(0, 2)
    def _(turn):
        b = 2 * turn + 1
        hand_out(b, sums[b] + against(b, far_columns), 0)

    for a in range(4):
        row_arrived(a, 2)
    hand_out(2, against(2, near_columns + far_columns), 0)
    total = sums[0] + against(0, far_columns)
    hand_out(0, total, 1)
    total = total[:, 0:OWN]
    for slot in range(1, 16):
        arrived(inbox.at[slot], out_recv.at[slot])
        total = total + inbox[slot].astype(jnp.float32)
    out_ref[...] = total

    for copy in started:
        copy.wait_send()
    for slot in range(1, 16):
        out_copy(slot % 4, slot // 4).wait_send()


def per_device(features, coeffs, targets):
    dma = pltpu.SemaphoreType.DMA
    predicted = pl.pallas_call(
        kernel,
        out_shape=jax.ShapeDtypeStruct((OUTS, OWN), jnp.float32),
        in_specs=[pl.BlockSpec(memory_space=pl.ANY)] * 2,
        out_specs=pl.BlockSpec(memory_space=pltpu.VMEM),
        scratch_shapes=[
            pltpu.VMEM((FEAT, OWN), jnp.bfloat16),
            pltpu.VMEM((OUTS, OWN), jnp.bfloat16),
            pltpu.VMEM((16, OWN, PAD), jnp.bfloat16),
            pltpu.VMEM((16, OUTS, OWN), jnp.bfloat16),
            pltpu.VMEM((16, PAD, OWN), jnp.bfloat16),
            pltpu.VMEM((16 * OWN, 4 * OWN), jnp.bfloat16),
            pltpu.VMEM((4, OUTS, 4 * OWN), jnp.float32),
            pltpu.VMEM((16, OUTS, OWN), jnp.bfloat16),
            pltpu.VMEM((16, OUTS, OWN), jnp.bfloat16),
            dma((2,)),
            dma((2, 4, PIECES)), dma((8, PIECES)),
            dma((8, 2)), dma((8, 2)),
            dma((4,)), dma((2, 4)), dma((4,)), dma((16,)),
            dma((16,)), dma((16,)),
        ],
        compiler_params=pltpu.CompilerParams(collective_id=0, has_side_effects=True, vmem_limit_bytes=32 << 20),
        name="ridge",
    )(pltpu.with_memory_space_constraint(features.T, pltpu.HBM), pltpu.with_memory_space_constraint(coeffs.T, pltpu.HBM))
    return predicted.T - targets


def solution(mesh):
    spec = P(("row", "col"), None)
    return jax.shard_map(per_device, mesh=mesh, in_specs=(spec, spec, spec), out_specs=spec, check_vma=False)
```

```python
import functools

import jax
import jax.numpy as jnp
from jax import lax
from jax.experimental import pallas as pl
from jax.experimental.pallas import tpu as pltpu
from jax.sharding import PartitionSpec as P

MESH = pl.DeviceIdType.MESH
NX, NY, NZ = 4, 4, 8
FEAT, OUTS, OWN = 440, 144, 128
PAD = 512
WIRE = 448
HEAD = 64
PIECES = 5
LOG2E = 1.4426950408889634
PLACES = (
    (0, 0), (1, 0), (2, 0), (3, 0),
    (0, 1), (1, 1), (0, 3), (3, 3),
    (2, 1), (3, 1), (2, 3), (1, 3),
    (0, 2), (1, 2), (2, 2), (3, 2),
)
SLOT = {place: slot for slot, place in enumerate(PLACES)}


def contract(a, b):
    return lax.dot_general(a, b, (((1,), (0,)), ((), ())), preferred_element_type=jnp.float32)


def laplacian(squared):
    squared = jnp.maximum(squared, 1e-30)
    return jnp.exp2((squared * -LOG2E) * lax.rsqrt(squared)).astype(jnp.bfloat16)


def kernel(
    feat_hbm, coef_hbm, out_ref,
    feat, coef, cols, weights, rows, gram, first_sums, sums, sent, inbox,
    load_sem, z_send, z_recv, chip_send, chip_recv, p_send, q_send, relay_send, row_recv, out_send, out_recv,
):
    row, col = lax.axis_index("row"), lax.axis_index("col")
    z, core = row // 4, row % 2
    x, y = (col % 2) * 2 + (row // 2) % 2, col // 2
    flip = 1 - core

    def device(x, y, z, core):
        return (z * 4 + (x % 2) * 2 + core, y * 2 + x // 2)

    def plane(a, b):
        return device((x + flip * a + core * b) % NX, (y + core * a + flip * b) % NY, z, core)

    def line(step):
        return device(x, y, (z + step + NZ) % NZ, core)

    sibling = device(x, y, z, flip)

    barrier = pltpu.get_barrier_semaphore()
    near = [line(1), line(-1), sibling, plane(1, 0), plane(3, 0), plane(2, 0), plane(0, 1), plane(0, 3)]
    for peer in near:
        pl.semaphore_signal(barrier, inc=1, device_id=peer, device_id_type=MESH)

    load_feat = pltpu.make_async_copy(feat_hbm, feat, load_sem.at[0])
    load_coef = pltpu.make_async_copy(coef_hbm, coef, load_sem.at[1])
    load_feat.start()
    load_coef.start()

    @pl.loop(1, 16)
    def _(slot):
        rows[slot, WIRE:PAD, :] = jnp.zeros((PAD - WIRE, OWN), jnp.bfloat16)

    load_feat.wait()
    load_coef.wait()

    values = feat[...].astype(jnp.float32)
    head = coef[0:HEAD, :].astype(jnp.float32)
    square = jnp.sum(values * values, axis=0, keepdims=True)
    first = square.astype(jnp.bfloat16).astype(jnp.float32)
    second = (square - first).astype(jnp.bfloat16).astype(jnp.float32)
    third = square - first - second
    at = lax.broadcasted_iota(jnp.int32, (8, OWN), 0)
    pieces = jnp.where(at % 3 == 0, first, jnp.where(at % 3 == 1, second, third))
    column_extra = jnp.where(at < 3, pieces, jnp.where(at < 6, 1.0, 0.0))
    row_extra = jnp.where(at < 3, 1.0, jnp.where(at < 6, pieces, 0.0))
    by_rows = jnp.concatenate([values, row_extra, jnp.zeros_like(head)], axis=0)
    rows[0] = by_rows.astype(jnp.bfloat16)
    by_columns = jnp.concatenate([values * -2.0, column_extra, head], axis=0)
    for t in range(4):
        cols[0, :, t * 128 : (t + 1) * 128] = jnp.transpose(by_columns[t * 128 : (t + 1) * 128]).astype(jnp.bfloat16)
    weights[0] = coef[...]

    pl.semaphore_wait(barrier, len(near))

    started = []

    def send(src, dst, send_sem, recv_sem, peer):
        copy = pltpu.make_async_remote_copy(
            src_ref=src, dst_ref=dst, send_sem=send_sem, recv_sem=recv_sem, device_id=peer, device_id_type=MESH
        )
        copy.start()
        started.append(copy)

    def arrived(dst, recv_sem):
        pltpu.make_async_remote_copy(
            src_ref=dst, dst_ref=dst, send_sem=load_sem.at[0], recv_sem=recv_sem, device_id=sibling, device_id_type=MESH
        ).wait_recv()

    def part(slot, piece):
        if piece < 4:
            return cols.at[slot, pl.ds(32 * piece, 32), :]
        return weights.at[slot, pl.ds(HEAD, OUTS - HEAD), :]

    def z_hop(step, piece, up):
        src = (8 - step + 1) % 8 if up else step - 1
        dst = 8 - step if up else step
        send(
            part(2 * src, piece), part(2 * dst, piece),
            z_send.at[int(up), step - 1, piece], z_recv.at[dst, piece], line(1 if up else -1),
        )

    def z_arrived(dz, piece):
        arrived(part(2 * dz, piece), z_recv.at[dz, piece])

    def to_sibling(dz):
        send(cols.at[2 * dz], cols.at[2 * dz + 1], chip_send.at[dz, 0], chip_recv.at[dz, 0], sibling)
        send(part(2 * dz, 4), part(2 * dz + 1, 4), chip_send.at[dz, 1], chip_recv.at[dz, 1], sibling)

    def from_sibling(dz):
        arrived(cols.at[2 * dz + 1], chip_recv.at[dz, 0])
        arrived(part(2 * dz + 1, 4), chip_recv.at[dz, 1])

    def row_block(a, b):
        return rows.at[SLOT[a, b], pl.ds(0, WIRE), :]

    def send_row(a, b, to_a, to_b, send_sem):
        there = ((a - to_a) % 4, (b - to_b) % 4)
        send(row_block(a, b), row_block(*there), send_sem, row_recv.at[SLOT[there]], plane(to_a, to_b))

    def row_arrived(a, b):
        arrived(row_block(a, b), row_recv.at[SLOT[a, b]])

    def across(a):
        send_row(a, 0, 0, 1, q_send.at[0, a])
        send_row(a, 0, 0, 3, q_send.at[1, a])

    def relay(a):
        if a < 2:
            row_arrived(a, 3)
            send_row(a, 3, 0, 1, relay_send.at[a])
        else:
            row_arrived(a, 1)
            send_row(a, 1, 0, 3, relay_send.at[a])

    def head_rows(slot):
        tail = jnp.transpose(cols[slot, :, 384:PAD].astype(jnp.float32))
        weights[slot, 0:HEAD, :] = tail[HEAD:128].astype(jnp.bfloat16)

    def against(group, distances):
        group = jnp.concatenate([rows[4 * group + i] for i in range(4)], axis=1)
        for at, dz in enumerate(distances):
            block = cols[2 * dz : 2 * dz + 2].reshape(2 * OWN, PAD)
            gram[2 * at * OWN : 2 * (at + 1) * OWN, :] = laplacian(contract(block, group))
        factors = jnp.concatenate([weights[2 * dz + half] for dz in distances for half in range(2)], axis=1)
        return contract(factors, gram[0 : 2 * len(distances) * OWN, :])

    for piece in range(PIECES):
        for up in (True, False):
            z_hop(1, piece, up)
    for a in (1, 3):
        send_row(0, 0, a, 0, p_send.at[a])
    send_row(0, 0, 2, 0, p_send.at[2])
    across(0)
    to_sibling(0)

    def z_round(step, pieces):
        for piece in pieces:
            for up in (True, False):
                z_arrived(8 - step if up else step, piece)
                if step < 3 or (step == 3 and (piece < 2) == up):
                    z_hop(step + 1, piece, up)

    z_round(1, range(5))
    to_sibling(1)
    to_sibling(7)
    for a in (1, 3):
        row_arrived(a, 0)
        across(a)
    relay(0)
    z_round(2, (0, 1))
    row_arrived(2, 0)
    across(2)
    z_round(2, (2,))
    from_sibling(0)
    head_rows(1)
    first_sums[...] = against(0, (0,))
    z_round(2, (3, 4))
    to_sibling(2)
    to_sibling(6)
    for dz in (1, 7):
        from_sibling(dz)
        head_rows(2 * dz)
        head_rows(2 * dz + 1)
    z_round(3, (0,))
    first_sums[...] += against(0, (1,))
    z_round(3, (1,))
    first_sums[...] += against(0, (7,))
    z_round(3, (2, 3, 4))
    to_sibling(3)
    to_sibling(5)
    relay(1)
    relay(3)
    relay(2)
    for dz in (2, 6):
        from_sibling(dz)
        head_rows(2 * dz)
        head_rows(2 * dz + 1)

    near_columns, far_columns = (0, 1, 7, 2, 6), (3, 5, 4)
    row_arrived(0, 1)
    row_arrived(1, 1)
    row_arrived(3, 3)

    sums[...] = against(1, near_columns)

    for piece in (0, 2, 1, 3, 4):
        z_arrived(4, piece)
    to_sibling(4)
    for dz in (3, 5):
        head_rows(2 * dz)
        from_sibling(dz)
        head_rows(2 * dz + 1)
    sums[...] += against(1, (3, 5))
    head_rows(8)
    from_sibling(4)
    head_rows(9)

    def out_copy(slot):
        return pltpu.make_async_remote_copy(
            src_ref=sent.at[slot], dst_ref=inbox.at[slot], send_sem=out_send.at[slot], recv_sem=out_recv.at[slot],
            device_id=plane(*PLACES[slot]), device_id_type=MESH,
        )

    def hand_out(group, total, first):
        for i in range(first, 4):
            sent[4 * group + i] = total[:, i * OWN : (i + 1) * OWN].astype(jnp.bfloat16)
        for i in range(first, 4):
            out_copy(4 * group + i).start()

    hand_out(1, sums[...] + against(1, (4,)), 0)
    row_arrived(2, 3)
    hand_out(2, against(2, near_columns + far_columns), 0)
    for a in range(4):
        row_arrived(a, 2)
    hand_out(3, against(3, near_columns + far_columns), 0)
    total = first_sums[...] + against(0, (2, 6) + far_columns)
    hand_out(0, total, 1)
    total = total[:, 0:OWN]
    for slot in (*range(4, 16), 1, 3, 2):
        arrived(inbox.at[slot], out_recv.at[slot])
        total = total + inbox[slot].astype(jnp.float32)
    out_ref[...] = total

    for copy in started:
        copy.wait_send()
    for slot in range(1, 16):
        out_copy(slot).wait_send()


def per_device(features, coeffs, targets):
    dma = pltpu.SemaphoreType.DMA
    predicted = pl.pallas_call(
        kernel,
        out_shape=jax.ShapeDtypeStruct((OUTS, OWN), jnp.float32),
        in_specs=[pl.BlockSpec(memory_space=pl.ANY)] * 2,
        out_specs=pl.BlockSpec(memory_space=pltpu.VMEM),
        scratch_shapes=[
            pltpu.VMEM((FEAT, OWN), jnp.bfloat16),
            pltpu.VMEM((OUTS, OWN), jnp.bfloat16),
            pltpu.VMEM((16, OWN, PAD), jnp.bfloat16),
            pltpu.VMEM((16, OUTS, OWN), jnp.bfloat16),
            pltpu.VMEM((16, PAD, OWN), jnp.bfloat16),
            pltpu.VMEM((16 * OWN, 4 * OWN), jnp.bfloat16),
            pltpu.VMEM((OUTS, 4 * OWN), jnp.float32),
            pltpu.VMEM((OUTS, 4 * OWN), jnp.float32),
            pltpu.VMEM((16, OUTS, OWN), jnp.bfloat16),
            pltpu.VMEM((16, OUTS, OWN), jnp.bfloat16),
            dma((2,)),
            dma((2, 4, PIECES)), dma((8, PIECES)),
            dma((8, 2)), dma((8, 2)),
            dma((4,)), dma((2, 4)), dma((4,)), dma((16,)),
            dma((16,)), dma((16,)),
        ],
        compiler_params=pltpu.CompilerParams(collective_id=0, has_side_effects=True, vmem_limit_bytes=32 << 20),
        name="ridge",
    )(pltpu.with_memory_space_constraint(features.T, pltpu.HBM), pltpu.with_memory_space_constraint(coeffs.T, pltpu.HBM))
    return predicted.T - targets


def solution(mesh):
    spec = P(("row", "col"), None)
    return jax.shard_map(per_device, mesh=mesh, in_specs=(spec, spec, spec), out_specs=spec, check_vma=False)
```

```python
import functools

import jax
import jax.numpy as jnp
from jax import lax
from jax.experimental import pallas as pl
from jax.experimental.pallas import tpu as pltpu
from jax.sharding import PartitionSpec as P

MESH = pl.DeviceIdType.MESH
NX, NY, NZ = 4, 4, 8
FEAT, OUTS, OWN = 440, 144, 128
PAD = 512
WIRE = 448
HEAD = 64
PIECES = 5
LOG2E = 1.4426950408889634
PLACES = (
    (0, 0), (1, 0), (2, 0), (3, 0),
    (0, 1), (1, 1), (0, 3), (3, 3),
    (2, 1), (3, 1), (2, 3), (1, 3),
    (0, 2), (1, 2), (2, 2), (3, 2),
)
SLOT = {place: slot for slot, place in enumerate(PLACES)}


def contract(a, b):
    return lax.dot_general(a, b, (((1,), (0,)), ((), ())), preferred_element_type=jnp.float32)


def laplacian(squared):
    squared = jnp.maximum(squared, 1e-30)
    return jnp.exp2((squared * -LOG2E) * lax.rsqrt(squared)).astype(jnp.bfloat16)


def kernel(
    feat_hbm, coef_hbm, out_ref,
    feat, coef, cols, weights, rows, gram, first_sums, sums, sent, inbox,
    load_sem, z_send, z_recv, chip_send, chip_recv, p_send, q_send, relay_send, row_recv, out_send, out_recv,
):
    row, col = lax.axis_index("row"), lax.axis_index("col")
    z, core = row // 4, row % 2
    x, y = (col % 2) * 2 + (row // 2) % 2, col // 2
    flip = 1 - core

    def device(x, y, z, core):
        return (z * 4 + (x % 2) * 2 + core, y * 2 + x // 2)

    def plane(a, b):
        return device((x + flip * a + core * b) % NX, (y + core * a + flip * b) % NY, z, core)

    def line(step):
        return device(x, y, (z + step + NZ) % NZ, core)

    sibling = device(x, y, z, flip)

    barrier = pltpu.get_barrier_semaphore()
    near = [line(1), line(-1), sibling, plane(1, 0), plane(3, 0), plane(2, 0), plane(0, 1), plane(0, 3)]
    for peer in near:
        pl.semaphore_signal(barrier, inc=1, device_id=peer, device_id_type=MESH)

    load_feat = pltpu.make_async_copy(feat_hbm, feat, load_sem.at[0])
    load_coef = pltpu.make_async_copy(coef_hbm, coef, load_sem.at[1])
    load_feat.start()
    load_coef.start()

    @pl.loop(1, 16)
    def _(slot):
        rows[slot, WIRE:PAD, :] = jnp.zeros((PAD - WIRE, OWN), jnp.bfloat16)

    load_feat.wait()
    load_coef.wait()

    values = feat[...].astype(jnp.float32)
    head = coef[0:HEAD, :].astype(jnp.float32)
    square = jnp.sum(values * values, axis=0, keepdims=True)
    first = square.astype(jnp.bfloat16).astype(jnp.float32)
    second = (square - first).astype(jnp.bfloat16).astype(jnp.float32)
    third = square - first - second
    at = lax.broadcasted_iota(jnp.int32, (8, OWN), 0)
    pieces = jnp.where(at % 3 == 0, first, jnp.where(at % 3 == 1, second, third))
    column_extra = jnp.where(at < 3, pieces, jnp.where(at < 6, 1.0, 0.0))
    row_extra = jnp.where(at < 3, 1.0, jnp.where(at < 6, pieces, 0.0))
    by_rows = jnp.concatenate([values, row_extra, jnp.zeros_like(head)], axis=0)
    rows[0] = by_rows.astype(jnp.bfloat16)
    by_columns = jnp.concatenate([values * -2.0, column_extra, head], axis=0)
    for t in range(4):
        cols[0, :, t * 128 : (t + 1) * 128] = jnp.transpose(by_columns[t * 128 : (t + 1) * 128]).astype(jnp.bfloat16)
    weights[0] = coef[...]

    pl.semaphore_wait(barrier, len(near))

    started = []

    def send(src, dst, send_sem, recv_sem, peer):
        copy = pltpu.make_async_remote_copy(
            src_ref=src, dst_ref=dst, send_sem=send_sem, recv_sem=recv_sem, device_id=peer, device_id_type=MESH
        )
        copy.start()
        started.append(copy)

    def arrived(dst, recv_sem):
        pltpu.make_async_remote_copy(
            src_ref=dst, dst_ref=dst, send_sem=load_sem.at[0], recv_sem=recv_sem, device_id=sibling, device_id_type=MESH
        ).wait_recv()

    def part(slot, piece):
        if piece < 4:
            return cols.at[slot, pl.ds(32 * piece, 32), :]
        return weights.at[slot, pl.ds(HEAD, OUTS - HEAD), :]

    def z_hop(step, piece, up):
        src = (8 - step + 1) % 8 if up else step - 1
        dst = 8 - step if up else step
        send(
            part(2 * src, piece), part(2 * dst, piece),
            z_send.at[int(up), step - 1, piece], z_recv.at[dst, piece], line(1 if up else -1),
        )

    def in_turn(turn, up):
        return turn if up else (turn + 2) % PIECES

    def z_arrived(dz, piece):
        arrived(part(2 * dz, piece), z_recv.at[dz, piece])

    def to_sibling(dz):
        send(cols.at[2 * dz], cols.at[2 * dz + 1], chip_send.at[dz, 0], chip_recv.at[dz, 0], sibling)
        send(part(2 * dz, 4), part(2 * dz + 1, 4), chip_send.at[dz, 1], chip_recv.at[dz, 1], sibling)

    def from_sibling(dz):
        arrived(cols.at[2 * dz + 1], chip_recv.at[dz, 0])
        arrived(part(2 * dz + 1, 4), chip_recv.at[dz, 1])

    def row_block(a, b):
        return rows.at[SLOT[a, b], pl.ds(0, WIRE), :]

    def send_row(a, b, to_a, to_b, send_sem):
        there = ((a - to_a) % 4, (b - to_b) % 4)
        send(row_block(a, b), row_block(*there), send_sem, row_recv.at[SLOT[there]], plane(to_a, to_b))

    def row_arrived(a, b):
        arrived(row_block(a, b), row_recv.at[SLOT[a, b]])

    def across(a):
        send_row(a, 0, 0, 1, q_send.at[0, a])
        send_row(a, 0, 0, 3, q_send.at[1, a])

    def relay(a):
        if a < 2:
            row_arrived(a, 3)
            send_row(a, 3, 0, 1, relay_send.at[a])
        else:
            row_arrived(a, 1)
            send_row(a, 1, 0, 3, relay_send.at[a])

    def head_rows(slot):
        tail = jnp.transpose(cols[slot, :, 384:PAD].astype(jnp.float32))
        weights[slot, 0:HEAD, :] = tail[HEAD:128].astype(jnp.bfloat16)

    def against(group, distances):
        group = jnp.concatenate([rows[4 * group + i] for i in range(4)], axis=1)
        for at, dz in enumerate(distances):
            block = cols[2 * dz : 2 * dz + 2].reshape(2 * OWN, PAD)
            gram[2 * at * OWN : 2 * (at + 1) * OWN, :] = laplacian(contract(block, group))
        factors = jnp.concatenate([weights[2 * dz + half] for dz in distances for half in range(2)], axis=1)
        return contract(factors, gram[0 : 2 * len(distances) * OWN, :])

    for turn in range(PIECES):
        for up in (True, False):
            z_hop(1, in_turn(turn, up), up)
    for a in (1, 3):
        send_row(0, 0, a, 0, p_send.at[a])
    send_row(0, 0, 2, 0, p_send.at[2])
    across(0)
    to_sibling(0)

    def z_round(step, turns):
        for turn in turns:
            for up in (True, False):
                piece = in_turn(turn, up)
                z_arrived(8 - step if up else step, piece)
                if step < 3 or (step == 3 and (piece < 2) == up):
                    z_hop(step + 1, piece, up)

    z_round(1, range(5))
    to_sibling(1)
    to_sibling(7)
    for a in (1, 3):
        row_arrived(a, 0)
        across(a)
    relay(0)
    z_round(2, (0, 1))
    row_arrived(2, 0)
    across(2)
    z_round(2, (2,))
    from_sibling(0)
    head_rows(1)
    first_sums[...] = against(0, (0,))
    z_round(2, (3, 4))
    to_sibling(2)
    to_sibling(6)
    for dz in (1, 7):
        from_sibling(dz)
        head_rows(2 * dz)
        head_rows(2 * dz + 1)
    z_round(3, (0, 1, 2))
    first_sums[...] += against(0, (1, 7))
    relay(1)
    relay(3)
    relay(2)
    for dz in (2, 6):
        from_sibling(dz)
        head_rows(2 * dz)
        head_rows(2 * dz + 1)
    z_round(3, (3, 4))
    to_sibling(3)
    to_sibling(5)

    near_columns, far_columns = (0, 1, 7, 2, 6), (3, 5, 4)
    row_arrived(0, 1)
    row_arrived(1, 1)
    row_arrived(3, 3)
    sums[...] = against(1, near_columns)

    for piece in (0, 2, 1, 3, 4):
        z_arrived(4, piece)
    to_sibling(4)
    for dz in (3, 5):
        head_rows(2 * dz)
        from_sibling(dz)
        head_rows(2 * dz + 1)
    sums[...] += against(1, (3, 5))
    head_rows(8)
    from_sibling(4)
    head_rows(9)

    def out_copy(slot):
        return pltpu.make_async_remote_copy(
            src_ref=sent.at[slot], dst_ref=inbox.at[slot], send_sem=out_send.at[slot], recv_sem=out_recv.at[slot],
            device_id=plane(*PLACES[slot]), device_id_type=MESH,
        )

    def hand_out(group, total, first):
        for i in range(first, 4):
            sent[4 * group + i] = total[:, i * OWN : (i + 1) * OWN].astype(jnp.bfloat16)
        for i in range(first, 4):
            out_copy(4 * group + i).start()

    hand_out(1, sums[...] + against(1, (4,)), 0)
    row_arrived(2, 3)
    hand_out(2, against(2, near_columns + far_columns), 0)
    for a in range(4):
        row_arrived(a, 2)
    hand_out(3, against(3, near_columns + far_columns), 0)
    total = first_sums[...] + against(0, (2, 6) + far_columns)
    hand_out(0, total, 1)
    total = total[:, 0:OWN]
    for slot in (*range(4, 16), 1, 3, 2):
        arrived(inbox.at[slot], out_recv.at[slot])
        total = total + inbox[slot].astype(jnp.float32)
    out_ref[...] = total

    for copy in started:
        copy.wait_send()
    for slot in range(1, 16):
        out_copy(slot).wait_send()


def per_device(features, coeffs, targets):
    dma = pltpu.SemaphoreType.DMA
    predicted = pl.pallas_call(
        kernel,
        out_shape=jax.ShapeDtypeStruct((OUTS, OWN), jnp.float32),
        in_specs=[pl.BlockSpec(memory_space=pl.ANY)] * 2,
        out_specs=pl.BlockSpec(memory_space=pltpu.VMEM),
        scratch_shapes=[
            pltpu.VMEM((FEAT, OWN), jnp.bfloat16),
            pltpu.VMEM((OUTS, OWN), jnp.bfloat16),
            pltpu.VMEM((16, OWN, PAD), jnp.bfloat16),
            pltpu.VMEM((16, OUTS, OWN), jnp.bfloat16),
            pltpu.VMEM((16, PAD, OWN), jnp.bfloat16),
            pltpu.VMEM((16 * OWN, 4 * OWN), jnp.bfloat16),
            pltpu.VMEM((OUTS, 4 * OWN), jnp.float32),
            pltpu.VMEM((OUTS, 4 * OWN), jnp.float32),
            pltpu.VMEM((16, OUTS, OWN), jnp.bfloat16),
            pltpu.VMEM((16, OUTS, OWN), jnp.bfloat16),
            dma((2,)),
            dma((2, 4, PIECES)), dma((8, PIECES)),
            dma((8, 2)), dma((8, 2)),
            dma((4,)), dma((2, 4)), dma((4,)), dma((16,)),
            dma((16,)), dma((16,)),
        ],
        compiler_params=pltpu.CompilerParams(collective_id=0, has_side_effects=True, vmem_limit_bytes=32 << 20),
        name="ridge",
    )(pltpu.with_memory_space_constraint(features.T, pltpu.HBM), pltpu.with_memory_space_constraint(coeffs.T, pltpu.HBM))
    return predicted.T - targets


def solution(mesh):
    spec = P(("row", "col"), None)
    return jax.shard_map(per_device, mesh=mesh, in_specs=(spec, spec, spec), out_specs=spec, check_vma=False)
```

```python
import functools

import jax
import jax.numpy as jnp
from jax import lax
from jax.experimental import pallas as pl
from jax.experimental.pallas import tpu as pltpu
from jax.sharding import PartitionSpec as P

MESH = pl.DeviceIdType.MESH
NX, NY, NZ = 4, 4, 8
FEAT, OUTS, OWN = 440, 144, 128
PAD = 512
WIRE = 448
HEAD = 64
PIECES = 5
LOG2E = 1.4426950408889634
PLACES = (
    (0, 0), (1, 0), (2, 0), (3, 0),
    (0, 1), (1, 1), (0, 3), (3, 3),
    (2, 1), (3, 1), (2, 3), (1, 3),
    (0, 2), (1, 2), (2, 2), (3, 2),
)
SLOT = {place: slot for slot, place in enumerate(PLACES)}


def contract(a, b):
    return lax.dot_general(a, b, (((1,), (0,)), ((), ())), preferred_element_type=jnp.float32)


def laplacian(squared):
    squared = jnp.maximum(squared, 1e-30)
    return jnp.exp2((squared * -LOG2E) * lax.rsqrt(squared)).astype(jnp.bfloat16)


def kernel(
    feat_hbm, coef_hbm, out_ref,
    feat, coef, cols, weights, rows, gram, first_sums, sums, sent, inbox,
    load_sem, z_send, z_recv, chip_send, chip_recv, p_send, q_send, relay_send, row_recv, out_send, out_recv, last_send, last_recv,
):
    row, col = lax.axis_index("row"), lax.axis_index("col")
    z, core = row // 4, row % 2
    x, y = (col % 2) * 2 + (row // 2) % 2, col // 2
    flip = 1 - core

    def device(x, y, z, core):
        return (z * 4 + (x % 2) * 2 + core, y * 2 + x // 2)

    def plane(a, b):
        return device((x + flip * a + core * b) % NX, (y + core * a + flip * b) % NY, z, core)

    def line(step):
        return device(x, y, (z + step + NZ) % NZ, core)

    sibling = device(x, y, z, flip)

    barrier = pltpu.get_barrier_semaphore()
    near = [line(1), line(-1), sibling, plane(1, 0), plane(3, 0), plane(2, 0), plane(0, 1), plane(0, 3)]
    for peer in near:
        pl.semaphore_signal(barrier, inc=1, device_id=peer, device_id_type=MESH)

    load_feat = pltpu.make_async_copy(feat_hbm, feat, load_sem.at[0])
    load_coef = pltpu.make_async_copy(coef_hbm, coef, load_sem.at[1])
    load_feat.start()
    load_coef.start()

    @pl.loop(1, 16)
    def _(slot):
        rows[slot, WIRE:PAD, :] = jnp.zeros((PAD - WIRE, OWN), jnp.bfloat16)

    load_feat.wait()
    load_coef.wait()

    values = feat[...].astype(jnp.float32)
    head = coef[0:HEAD, :].astype(jnp.float32)
    square = jnp.sum(values * values, axis=0, keepdims=True)
    first = square.astype(jnp.bfloat16).astype(jnp.float32)
    second = (square - first).astype(jnp.bfloat16).astype(jnp.float32)
    third = square - first - second
    at = lax.broadcasted_iota(jnp.int32, (8, OWN), 0)
    pieces = jnp.where(at % 3 == 0, first, jnp.where(at % 3 == 1, second, third))
    column_extra = jnp.where(at < 3, pieces, jnp.where(at < 6, 1.0, 0.0))
    row_extra = jnp.where(at < 3, 1.0, jnp.where(at < 6, pieces, 0.0))
    by_rows = jnp.concatenate([values, row_extra, jnp.zeros_like(head)], axis=0)
    rows[0] = by_rows.astype(jnp.bfloat16)
    by_columns = jnp.concatenate([values * -2.0, column_extra, head], axis=0)
    for t in range(4):
        cols[0, :, t * 128 : (t + 1) * 128] = jnp.transpose(by_columns[t * 128 : (t + 1) * 128]).astype(jnp.bfloat16)
    weights[0] = coef[...]

    pl.semaphore_wait(barrier, len(near))

    started = []

    def send(src, dst, send_sem, recv_sem, peer):
        copy = pltpu.make_async_remote_copy(
            src_ref=src, dst_ref=dst, send_sem=send_sem, recv_sem=recv_sem, device_id=peer, device_id_type=MESH
        )
        copy.start()
        started.append(copy)

    def arrived(dst, recv_sem):
        pltpu.make_async_remote_copy(
            src_ref=dst, dst_ref=dst, send_sem=load_sem.at[0], recv_sem=recv_sem, device_id=sibling, device_id_type=MESH
        ).wait_recv()

    def part(slot, piece):
        if piece < 4:
            return cols.at[slot, pl.ds(32 * piece, 32), :]
        return weights.at[slot, pl.ds(HEAD, OUTS - HEAD), :]

    def z_hop(step, piece, up):
        src = (8 - step + 1) % 8 if up else step - 1
        dst = 8 - step if up else step
        send(
            part(2 * src, piece), part(2 * dst, piece),
            z_send.at[int(up), step - 1, piece], z_recv.at[dst, piece], line(1 if up else -1),
        )

    def in_turn(turn, up):
        return turn if up else (turn + 2) % PIECES

    def z_arrived(dz, piece):
        arrived(part(2 * dz, piece), z_recv.at[dz, piece])

    def to_sibling(dz):
        send(cols.at[2 * dz], cols.at[2 * dz + 1], chip_send.at[dz, 0], chip_recv.at[dz, 0], sibling)
        send(part(2 * dz, 4), part(2 * dz + 1, 4), chip_send.at[dz, 1], chip_recv.at[dz, 1], sibling)

    def from_sibling(dz):
        arrived(cols.at[2 * dz + 1], chip_recv.at[dz, 0])
        arrived(part(2 * dz + 1, 4), chip_recv.at[dz, 1])

    def row_block(a, b):
        return rows.at[SLOT[a, b], pl.ds(0, WIRE), :]

    def send_row(a, b, to_a, to_b, send_sem):
        there = ((a - to_a) % 4, (b - to_b) % 4)
        send(row_block(a, b), row_block(*there), send_sem, row_recv.at[SLOT[there]], plane(to_a, to_b))

    def row_arrived(a, b):
        arrived(row_block(a, b), row_recv.at[SLOT[a, b]])

    def across(a):
        send_row(a, 0, 0, 1, q_send.at[0, a])
        send_row(a, 0, 0, 3, q_send.at[1, a])

    def relay(a):
        if a < 2:
            row_arrived(a, 3)
            send_row(a, 3, 0, 1, relay_send.at[a])
        else:
            row_arrived(a, 1)
            send_row(a, 1, 0, 3, relay_send.at[a])

    def head_rows(slot):
        tail = jnp.transpose(cols[slot, :, 384:PAD].astype(jnp.float32))
        weights[slot, 0:HEAD, :] = tail[HEAD:128].astype(jnp.bfloat16)

    def against(group, distances):
        group = jnp.concatenate([rows[4 * group + i] for i in range(4)], axis=1)
        for at, dz in enumerate(distances):
            block = cols[2 * dz : 2 * dz + 2].reshape(2 * OWN, PAD)
            gram[2 * at * OWN : 2 * (at + 1) * OWN, :] = laplacian(contract(block, group))
        factors = jnp.concatenate([weights[2 * dz + half] for dz in distances for half in range(2)], axis=1)
        return contract(factors, gram[0 : 2 * len(distances) * OWN, :])

    for turn in range(PIECES):
        for up in (True, False):
            z_hop(1, in_turn(turn, up), up)
    for a in (1, 3):
        send_row(0, 0, a, 0, p_send.at[a])
    send_row(0, 0, 2, 0, p_send.at[2])
    across(0)
    to_sibling(0)

    def z_round(step, turns):
        for turn in turns:
            for up in (True, False):
                piece = in_turn(turn, up)
                z_arrived(8 - step if up else step, piece)
                if step < 3 or (step == 3 and (piece < 2) == up):
                    z_hop(step + 1, piece, up)

    z_round(1, range(5))
    to_sibling(1)
    to_sibling(7)
    for a in (1, 3):
        row_arrived(a, 0)
        across(a)
    relay(0)
    z_round(2, (0, 1))
    row_arrived(2, 0)
    across(2)
    z_round(2, (2,))
    from_sibling(0)
    head_rows(1)
    first_sums[...] = against(0, (0,))
    z_round(2, (3, 4))
    to_sibling(2)
    to_sibling(6)
    for dz in (1, 7):
        from_sibling(dz)
        head_rows(2 * dz)
        head_rows(2 * dz + 1)
    z_round(3, (0, 1, 2))
    first_sums[...] += against(0, (1, 7))
    relay(1)
    relay(3)
    relay(2)
    for dz in (2, 6):
        from_sibling(dz)
        head_rows(2 * dz)
        head_rows(2 * dz + 1)
    z_round(3, (3, 4))
    to_sibling(3)
    to_sibling(5)

    near_columns, far_columns = (0, 1, 7, 2, 6), (3, 5, 4)
    row_arrived(0, 1)
    row_arrived(1, 1)
    row_arrived(3, 3)
    sums[...] = against(1, near_columns)

    for piece in (0, 2, 1, 3, 4):
        z_arrived(4, piece)
        send(part(8, piece), part(9, piece), last_send.at[piece], last_recv.at[piece], sibling)
    for dz in (3, 5):
        head_rows(2 * dz)
        from_sibling(dz)
        head_rows(2 * dz + 1)
    sums[...] += against(1, (3, 5))
    head_rows(8)
    for piece in range(PIECES):
        arrived(part(9, piece), last_recv.at[piece])
    head_rows(9)

    def out_copy(slot):
        return pltpu.make_async_remote_copy(
            src_ref=sent.at[slot], dst_ref=inbox.at[slot], send_sem=out_send.at[slot], recv_sem=out_recv.at[slot],
            device_id=plane(*PLACES[slot]), device_id_type=MESH,
        )

    def hand_out(group, total, first):
        for i in range(first, 4):
            sent[4 * group + i] = total[:, i * OWN : (i + 1) * OWN].astype(jnp.bfloat16)
        for i in range(first, 4):
            out_copy(4 * group + i).start()

    hand_out(1, sums[...] + against(1, (4,)), 0)
    row_arrived(2, 3)
    hand_out(2, against(2, near_columns + far_columns), 0)
    for a in range(4):
        row_arrived(a, 2)
    hand_out(3, against(3, near_columns + far_columns), 0)
    total = first_sums[...] + against(0, (2, 6) + far_columns)
    hand_out(0, total, 1)
    total = total[:, 0:OWN]
    for slot in (*range(4, 16), 1, 3, 2):
        arrived(inbox.at[slot], out_recv.at[slot])
        total = total + inbox[slot].astype(jnp.float32)
    out_ref[...] = total

    for copy in started:
        copy.wait_send()
    for slot in range(1, 16):
        out_copy(slot).wait_send()


def per_device(features, coeffs, targets):
    dma = pltpu.SemaphoreType.DMA
    predicted = pl.pallas_call(
        kernel,
        out_shape=jax.ShapeDtypeStruct((OUTS, OWN), jnp.float32),
        in_specs=[pl.BlockSpec(memory_space=pl.ANY)] * 2,
        out_specs=pl.BlockSpec(memory_space=pltpu.VMEM),
        scratch_shapes=[
            pltpu.VMEM((FEAT, OWN), jnp.bfloat16),
            pltpu.VMEM((OUTS, OWN), jnp.bfloat16),
            pltpu.VMEM((16, OWN, PAD), jnp.bfloat16),
            pltpu.VMEM((16, OUTS, OWN), jnp.bfloat16),
            pltpu.VMEM((16, PAD, OWN), jnp.bfloat16),
            pltpu.VMEM((16 * OWN, 4 * OWN), jnp.bfloat16),
            pltpu.VMEM((OUTS, 4 * OWN), jnp.float32),
            pltpu.VMEM((OUTS, 4 * OWN), jnp.float32),
            pltpu.VMEM((16, OUTS, OWN), jnp.bfloat16),
            pltpu.VMEM((16, OUTS, OWN), jnp.bfloat16),
            dma((2,)),
            dma((2, 4, PIECES)), dma((8, PIECES)),
            dma((8, 2)), dma((8, 2)),
            dma((4,)), dma((2, 4)), dma((4,)), dma((16,)),
            dma((16,)), dma((16,)),
            dma((PIECES,)), dma((PIECES,)),
        ],
        compiler_params=pltpu.CompilerParams(collective_id=0, has_side_effects=True, vmem_limit_bytes=32 << 20),
        name="ridge",
    )(pltpu.with_memory_space_constraint(features.T, pltpu.HBM), pltpu.with_memory_space_constraint(coeffs.T, pltpu.HBM))
    return predicted.T - targets


def solution(mesh):
    spec = P(("row", "col"), None)
    return jax.shard_map(per_device, mesh=mesh, in_specs=(spec, spec, spec), out_specs=spec, check_vma=False)
```
